32 devices in a mesh: rep: 4 (over x, core), dom: 8 (over z, y).
Axes of the slice: x: 2, y: 2, z: 4, core: 2. Of those that a mesh axis runs over, the one named last changes fastest.
Arguments:
- positions: float32 [3, 262144], P(None, ('rep', 'dom')), parts along dimension 1, may hold values from -4 to 4
- velocities: float32 [3, 262144], P(None, ('rep', 'dom')), parts along dimension 1, may hold values from -5 to 5
- charges: float32 [262144], P(('rep', 'dom')), parts along dimension 0, may hold values from -4 to 4
- solute: int32 [262144], P(('rep', 'dom')), parts along dimension 0, may hold values 0 or 1
- rest_scale: float32 [4], P('rep'), parts along dimension 0, may hold values from 0.25 to 1
- send_slot: int32 [32, 8], P(('rep', 'dom')), parts along dimension 0, may hold values from 0 to 64, as said below
- land_slot: int32 [32, 8], P(('rep', 'dom')), parts along dimension 0, may hold values from 0 to 64, as said below
- ghost_slot: int32 [32, 64], P(('rep', 'dom')), parts along dimension 0, may hold values from 0 to 63
- pair_home: int32 [32, 192], P(('rep', 'dom')), parts along dimension 0, may hold values from 0 to 63
- pair_other: int32 [32, 192], P(('rep', 'dom')), parts along dimension 0, may hold values from 0 to 127, as said below
Outputs:
- positions_out: float32 [3, 262144], P(None, ('rep', 'dom')), parts along dimension 1
- velocities_out: float32 [3, 262144], P(None, ('rep', 'dom')), parts along dimension 1
- forces_out: float32 [3, 262144], P(None, ('rep', 'dom')), parts along dimension 1
The draws below stay inside these ranges and needn't reach their ends.
There are 4 independent parts, one for each index of `rep`. The reference program is written for one: setup_inputs(seed, part) draws one part's arguments, and reference() takes and returns one part's arrays. A program takes and returns all parts, laid end to end along the dimension named above; each array names one. Nothing has to cross between parts.
Inputs may be any that keep to these rules, and one draw needn't show every extreme that they name: `send_slot`: entry [d, p] is the slot of the block domain d hands to domain p, or 64 where it hands none; each domain hands 4 distinct blocks to 4 distinct other domains, and each domain receives from 4 domains. `land_slot`: entry [d, p] is the slot that the block arriving at d from p takes, or 64 exactly where send_slot[p, d] is 64; the slots a domain fills are exactly the slots it hands over. `pair_other`: in every row the first 128 entries are below 64; the other 64 are 64 or more, and every ghost slot appears among them at least once.
All inputs are finite; a program needn't handle non-finite values. No bound on the sum of `solute` on one device may be relied on, other than what follows from the above.
Results may differ from the reference program's by a relative error of at most 0.0001.
Values sent between devices are 32-bit elements; how exact they have to be, the bound alone decides.
A program may use at most 64 MiB of HBM per device.

```python
import math
import jax
import jax.numpy as jnp
from jax import lax

BLOCK = 128
B_DEV = 64
STEPS = 2
MOVE = 4
GHOST_DEV = 64
GCAP = 8
LPAIRS = 128
GPAIRS = 64
PAIRS = 192
ATOMS = 65536
N_DOM = 8


def migration_plan(key):
    base = jax.random.fold_in(key, 17)
    first_key, second_key, third_key = jax.random.split(base, 3)
    offsets = 1 + jax.random.permutation(first_key, N_DOM - 1)[:MOVE]
    order_map = jax.random.permutation(second_key, N_DOM)
    inverse = jnp.argsort(order_map, stable=True)
    slots = jax.vmap(lambda subkey: jax.random.permutation(subkey, B_DEV)[:MOVE])(jax.random.split(third_key, N_DOM))
    domains = jnp.arange(N_DOM, dtype=jnp.int32)
    position = inverse[domains][:, None]
    destination = order_map[(position + offsets[None, :]) % N_DOM]
    anchor = order_map[(position - offsets[None, :]) % N_DOM]
    vacant = jnp.full((N_DOM, N_DOM), B_DEV, jnp.int32)
    handed = vacant.at[domains[:, None], destination].set(slots.astype(jnp.int32))
    landing = vacant.at[domains[:, None], anchor].set(slots.astype(jnp.int32))
    return (handed, landing)


def draw_send_slot(key, part):
    return migration_plan(key)[0]


def draw_land_slot(key, part):
    return migration_plan(key)[1]


def draw_pair_other(key, part):
    base = jax.random.fold_in(key, 29)
    first_key, second_key, third_key = jax.random.split(base, 3)
    nearby = jax.random.randint(first_key, (N_DOM, LPAIRS), 0, B_DEV)
    extra = jax.random.randint(second_key, (N_DOM, GPAIRS - GHOST_DEV), 0, GHOST_DEV)
    covered = jnp.broadcast_to(jnp.arange(GHOST_DEV, dtype=jnp.int32), (N_DOM, GHOST_DEV))
    chosen = jnp.concatenate([covered, extra.astype(jnp.int32)], 1)
    shuffled = jax.vmap(lambda subkey, entries: jax.random.permutation(subkey, entries))(jax.random.split(third_key, N_DOM), chosen)
    return jnp.concatenate([nearby.astype(jnp.int32), B_DEV + shuffled], 1).astype(jnp.int32)


def with_ends(values, stream_key, least, top_value):
    longest = values.shape.index(max(values.shape))
    spots = []
    for shift in (0, 1):
        where = [jax.random.randint(jax.random.fold_in(stream_key, axis), (), 0, length) for axis, length in enumerate(values.shape)]
        where[longest] = (where[longest] + shift) % values.shape[longest]
        spots.append(tuple(where))
    return values.at[spots[0]].set(least).at[spots[1]].set(top_value)


def block_levels(rng, extent, cuts, smallest, largest):
    gain = 1.0
    for dim, shards_of in cuts:
        heights = jax.random.uniform(jax.random.fold_in(jax.random.fold_in(rng, 6), dim), (shards_of,), jnp.float32, smallest / len(cuts), largest / len(cuts))
        gain = gain * jnp.repeat(jnp.exp(heights), extent[dim] // shards_of).reshape((-1,) + (1,) * (len(extent) - 1 - dim))
    return gain


def scatter_about(stream_key, shape, spread, limit, cuts=(), kind=jnp.bfloat16):
    drawn = jax.random.normal(stream_key, shape, jnp.float32) * spread
    if len(cuts) > 0:
        drawn = block_levels(stream_key, shape, cuts, -0.22, 0.18) * drawn
    return jnp.clip(drawn, min=-limit, max=limit).astype(kind)


def setup_inputs(seed: int = 0, part: int = 0) -> dict:
    key_of = jax.random.split(jax.random.key(seed), 11)
    part_keys = jax.random.split(jax.random.fold_in(key_of[10], part), 11)
    return {
        "positions": scatter_about(part_keys[0], (3, ATOMS), 1.0, 4.0, ((1, 8),), jnp.float32),
        "velocities": scatter_about(part_keys[1], (3, ATOMS), 1.0, 5.0, ((1, 8),), jnp.float32),
        "charges": scatter_about(part_keys[2], (ATOMS,), 1.0, 4.0, ((0, 8),), jnp.float32),
        "solute": with_ends((jax.random.randint(part_keys[3], (ATOMS,), 0, 5) < 2).astype(jnp.int32), jax.random.fold_in(part_keys[3], 1), 0, 1),
        "rest_scale": jnp.clip(jnp.exp(jax.random.uniform(part_keys[4], (1,), jnp.float32, math.log(0.25), math.log(1.0))), 0.25, 1.0),
        "send_slot": draw_send_slot(jax.random.fold_in(jax.random.fold_in(key_of[10], part), 71), part),
        "land_slot": draw_land_slot(jax.random.fold_in(jax.random.fold_in(key_of[10], part), 71), part),
        "ghost_slot": with_ends(jax.random.randint(part_keys[7], (N_DOM, GHOST_DEV), 0, B_DEV), jax.random.fold_in(part_keys[7], 1), 0, B_DEV - 1).astype(jnp.int32),
        "pair_home": with_ends(jax.random.randint(part_keys[8], (N_DOM, PAIRS), 0, B_DEV), jax.random.fold_in(part_keys[8], 1), 0, B_DEV - 1).astype(jnp.int32),
        "pair_other": draw_pair_other(jax.random.fold_in(jax.random.fold_in(key_of[10], part), 71), part),
    }


coupling_scale = 0.2
time_step = 0.05
highest = lax.Precision.HIGHEST

def tile_forces(left_coords, left_params, right_coords, right_params):
    inner = lax.dot_general(left_coords, right_coords, (((0,), (0,)), ((), ())), precision=highest, preferred_element_type=jnp.float32)
    squared = lax.optimization_barrier(jnp.sum(left_coords * left_coords, 0))[:, None] + lax.optimization_barrier(jnp.sum(right_coords * right_coords, 0))[None, :] - 2.0 * inner
    decay = jnp.exp(-0.5 * squared)
    coupling = coupling_scale * (left_params[0][:, None] * right_params[0][None, :] * decay + left_params[1][:, None] * right_params[1][None, :] * decay * decay)
    left_force = left_coords * lax.optimization_barrier(jnp.sum(coupling, 1))[None, :] - lax.dot_general(right_coords, coupling, (((1,), (1,)), ((), ())), precision=highest, preferred_element_type=jnp.float32)
    right_force = right_coords * lax.optimization_barrier(jnp.sum(coupling, 0))[None, :] - jnp.dot(left_coords, coupling, precision=highest, preferred_element_type=jnp.float32)
    return (left_force, right_force)

def all_forces(coords, params, home_ids, other_ids):

    def one_group(indices):
        home_rows, other_rows = indices
        return jax.vmap(tile_forces)(coords[home_rows], params[home_rows], coords[other_rows], params[other_rows])
    shaped = (home_ids.reshape(-1, 64), other_ids.reshape(-1, 64))
    home_force, other_force = lax.map(one_group, shaped)
    totals = jnp.zeros_like(coords)
    totals = totals.at[home_ids].add(home_force.reshape((-1,) + coords.shape[1:]))
    return totals.at[other_ids].add(other_force.reshape((-1,) + coords.shape[1:]))

def reference(positions, velocities, charges, solute, rest_scale, send_slot, land_slot, ghost_slot, pair_home, pair_other):
    weight = jnp.where(solute == 1, jnp.sqrt(rest_scale[0]), 1.0).astype(jnp.float32)
    params = jnp.stack([weight * charges, weight])
    states = jnp.concatenate([positions, velocities, params], 0)
    states = states.reshape(8, N_DOM * B_DEV, BLOCK).transpose(1, 0, 2).reshape(N_DOM, B_DEV, 8, BLOCK)
    domains = jnp.arange(N_DOM, dtype=jnp.int32)
    padded = jnp.concatenate([states, jnp.zeros((N_DOM, 1, 8, BLOCK), states.dtype)], 1)
    incoming = send_slot.T
    moved = padded[domains[None, :], incoming]
    placed = padded.at[domains[:, None], land_slot].set(moved)[:, :B_DEV]
    placed = placed.reshape(N_DOM * B_DEV, 8, BLOCK)
    ghost_index = jnp.maximum(pair_other - B_DEV, 0)
    source = (ghost_index // GCAP).astype(jnp.int32)
    within = (ghost_index % GCAP).astype(jnp.int32)
    remote = ghost_slot[source, domains[:, None] * GCAP + within]
    other_ids = jnp.where(pair_other < B_DEV, domains[:, None] * B_DEV + pair_other, source * B_DEV + remote).astype(jnp.int32).reshape(-1)
    home_ids = (domains[:, None] * B_DEV + pair_home).astype(jnp.int32).reshape(-1)
    coords = placed[:, :3]
    speeds = placed[:, 3:6]
    params_now = placed[:, 6:]
    forces = jnp.zeros_like(coords)
    for step_index in range(STEPS):
        forces = all_forces(coords, params_now, home_ids, other_ids)
        speeds = speeds + time_step * forces
        coords = coords + time_step * speeds

    def flatten(values):
        return values.transpose(1, 0, 2).reshape(3, N_DOM * B_DEV * BLOCK)
    return (flatten(coords), flatten(speeds), flatten(forces))
```

```python
import functools
import math

import jax
import jax.numpy as jnp
from jax import lax
from jax.experimental import pallas as pl
from jax.experimental.pallas import tpu as pltpu
from jax.sharding import PartitionSpec as P

BLOCK = 128
STEPS = 2
UNROLL = 4
TABLE_UNROLL = 16
PAIR_UNROLL = 32
AHEAD = 6
ROWS = 8
DEPTH = 48

coupling_scale = 0.2
time_step = 0.05
log2e = math.log2(math.e)
f32 = jnp.float32
bf16 = jnp.bfloat16
MESH = pl.DeviceIdType.MESH


def split(value):
    high = value.astype(bf16).astype(f32)
    rest = value - high
    middle = rest.astype(bf16).astype(f32)
    return high, middle, rest - middle


def nn(left, right):
    return lax.dot_general(left, right, (((1,), (0,)), ((), ())), preferred_element_type=f32)


def nt(left, right):
    return lax.dot_general(left, right, (((1,), (1,)), ((), ())), preferred_element_type=f32)


def kernel(
    n,
    blocks,
    ghosts,
    padded,
    pairs,
    home_ref,
    other_ref,
    send_ref,
    land_ref,
    slot_ref,
    scale_ref,
    home_vector,
    other_vector,
    slots_vector,
    pos_ref,
    vel_ref,
    charge_ref,
    solute_ref,
    pos_out,
    vel_out,
    force_out,
    old,
    tiles,
    state,
    move_out,
    move_in,
    ghost_out,
    ghost_in,
    force_send,
    force_recv,
    left_table,
    right_table,
    weighted,
    charge_rows,
    charge_wide,
    results,
    force_rows,
    source,
    send_sem,
    recv_sem,
):
    me = lax.axis_index("dom")
    group = ghosts // n
    local = pairs - ghosts
    total = n * padded
    row = lax.broadcasted_iota(jnp.int32, (ROWS, BLOCK), 0)

    barrier = pltpu.get_barrier_semaphore()

    def greet(j, carry):
        pl.semaphore_signal(barrier, inc=1, device_id={"dom": lax.rem(me + j, n)}, device_id_type=MESH)
        return carry

    lax.fori_loop(1, n, greet, 0)

    root = jnp.sqrt(jnp.full((1, BLOCK), scale_ref[0], f32))

    def gather_state(b, carry):
        lanes = pl.ds(pl.multiple_of(b * BLOCK, BLOCK), BLOCK)
        weight = jnp.where(solute_ref[pl.ds(b, 1), :] == 1, root, 1.0)
        old[b] = jnp.concatenate(
            [pos_ref[:, lanes], vel_ref[:, lanes], charge_ref[pl.ds(b, 1), :], weight], 0
        )
        return carry

    lax.fori_loop(0, blocks, gather_state, 0, unroll=UNROLL)

    def pack_move(j, carry):
        target = lax.rem(me + j, n)
        move_out[target] = old[jnp.minimum(send_ref[0, target], blocks - 1)]
        return carry

    lax.fori_loop(1, n, pack_move, 0)
    pl.semaphore_wait(barrier, n - 1)

    def exchange(phase, outgoing, incoming, size):
        def push(j, carry):
            target = lax.rem(me + j, n)
            pltpu.make_async_remote_copy(
                src_ref=outgoing.at[pl.ds(target * size, size)],
                dst_ref=incoming.at[pl.ds(me * size, size)],
                send_sem=send_sem.at[phase],
                recv_sem=recv_sem.at[phase],
                device_id={"dom": target},
                device_id_type=MESH,
            ).start()
            return carry

        lax.fori_loop(1, n, push, 0)

    def settle(sem, buffer, size):
        part = buffer.at[pl.ds(0, (n - 1) * size)]
        pltpu.make_async_copy(part, part, sem).wait()

    def rows_of(r, start, count):
        return pl.ds(start * ROWS + r, count, stride=ROWS)

    def tile_of(at):
        return pl.ds(pl.multiple_of(at * ROWS, ROWS), ROWS)

    exchange(0, move_out, move_in, 1)

    def find(s, carry):
        def look(p, best):
            return jnp.where(land_ref[0, p] == s, blocks + p, best)

        source[s] = lax.fori_loop(0, n, look, s, unroll=8)
        return carry

    lax.fori_loop(0, blocks, find, 0, unroll=UNROLL)
    settle(recv_sem.at[0], move_in, 1)

    def unpack(j, carry):
        origin = lax.rem(me + j, n)
        old[blocks + origin] = move_in[origin]
        return carry

    lax.fori_loop(1, n, unpack, 0)

    def place(s, carry):
        tile = old[source[s]]
        tiles[s] = tile
        state[tile_of(s), :] = tile
        return carry

    lax.fori_loop(0, blocks, place, 0, unroll=UNROLL)

    def partner_tables(tile, at):
        squares = jnp.where(row < 3, tile * tile, 0.0)
        norm = (-0.5 * log2e) * jnp.sum(squares, 0, keepdims=True)
        charge = tile[6:7]
        weight = tile[7:8]
        right = jnp.where(
            row < 3, log2e * tile, jnp.where(row == 3, 1.0, jnp.where(row == 4, norm, 0.0))
        )
        high, middle, low = split(right)
        right_table[at] = jnp.concatenate([high, middle, high, middle, low, high], 0).astype(bf16)
        scaled = jnp.where(row < 3, weight * tile, jnp.where(row == 3, weight, 0.0))
        high, middle, low = split(scaled)
        first = jnp.where(row < 4, high, pltpu.roll(low, 4, 0))
        weighted[at] = jnp.concatenate([first, middle], 0).astype(bf16)
        charge_rows[at] = jnp.broadcast_to(charge, (ROWS, BLOCK))
        return norm, charge

    deep = lax.broadcasted_iota(jnp.int32, (DEPTH, BLOCK), 0)
    picks = jnp.where((deep == 5) | (deep == 21) | (deep == 45), 1.0, 0.0).astype(bf16)

    def home_tables(first_step):
        def one(b, carry):
            tile = state[tile_of(b), :]
            norm, charge = partner_tables(tile, b)
            left = jnp.where(
                row < 3,
                tile,
                jnp.where(
                    row == 3,
                    norm,
                    jnp.where(row == 4, 1.0, jnp.where(row == 5, charge, 0.0)),
                ),
            )
            high, middle, low = split(left)
            stacked = jnp.concatenate([high, high, middle, middle, high, low], 0)
            turned = stacked.T.astype(bf16)
            left_table[b] = turned
            if first_step:
                charge_wide[b] = nn(turned, picks)
            return carry

        lax.fori_loop(0, blocks, one, 0, unroll=TABLE_UNROLL)

    def exponent_of(t):
        return nn(left_table[home_ref[0, t]], right_table[other_ref[0, t]])

    def finish_pair(t, exponent):
        home = home_ref[0, t]
        other = other_ref[0, t]
        decay = jnp.exp2(exponent)
        wide = charge_wide[home].reshape(BLOCK // ROWS, ROWS, BLOCK)
        charges = (wide * charge_rows[other][None]).reshape(BLOCK, BLOCK)
        coupling = decay * (charges + decay)
        high = coupling.astype(bf16)
        low = (coupling - high.astype(f32)).astype(bf16)
        both = jnp.concatenate([high, low], 1)
        home_rows = weighted[home]
        other_rows = weighted[other]
        to_other = nn(home_rows, both)
        to_home = nt(jnp.concatenate([other_rows, other_rows], 1), both)
        halves = to_other[:ROWS] + to_other[ROWS:]
        results[tile_of(t), :] = to_home[:ROWS] + to_home[ROWS:]
        results[tile_of(pairs + t), :] = halves[:, :BLOCK] + halves[:, BLOCK:]

    def run_pairs(start, stop):
        def some(i, carry):
            base = start + i * PAIR_UNROLL
            ahead = [exponent_of(base + u) for u in range(AHEAD)]
            for u in range(PAIR_UNROLL):
                if u + AHEAD < PAIR_UNROLL:
                    ahead.append(exponent_of(base + u + AHEAD))
                finish_pair(base + u, ahead[u])
            return carry

        lax.fori_loop(0, (stop - start) // PAIR_UNROLL, some, 0)

    def gathered(onehot, start):
        sums = []
        for r in range(4):
            value = (
                results[rows_of(r, start, pairs), :] + results[rows_of(r + 4, start, pairs), :]
            )
            high, middle, low = split(value)
            sums.append(
                nn(onehot, high.astype(bf16))
                + nn(onehot, middle.astype(bf16))
                + nn(onehot, low.astype(bf16))
            )
        return sums

    def onehot_of(count, indices, base):
        shape = (count, indices.shape[1])
        hit = lax.broadcasted_iota(jnp.int32, shape, 0) + base == indices
        return jnp.where(hit, 1.0, 0.0).astype(bf16)

    results[...] = jnp.zeros_like(results)

    for step in range(STEPS):
        fill = 1 + 2 * step
        back = fill + 1
        ghost_send = ghost_out.at[step]
        ghost_recv = ghost_in.at[step]
        sent = force_send.at[step]
        got = force_recv.at[step]
        span = padded * ROWS
        if padded != group:
            ghost_send[...] = jnp.zeros((n * span, BLOCK), f32)

        def pack(j, carry):
            target = lax.rem(me + j, n)
            for k in range(group):
                ghost_send[tile_of(target * padded + k), :] = tiles[
                    slot_ref[0, target * group + k]
                ]
            return carry

        lax.fori_loop(0, n, pack, 0)
        exchange(fill, ghost_send, ghost_recv, span)
        mine = pl.ds(pl.multiple_of(me * span, span), span)
        ghost_recv[mine, :] = ghost_send[mine, :]
        home_tables(step == 0)
        run_pairs(local // 2, local)
        settle(recv_sem.at[fill], ghost_recv, span)

        def ghost_tables(g, carry):
            partner_tables(ghost_recv[tile_of(g), :], blocks + g)
            return carry

        lax.fori_loop(0, total, ghost_tables, 0, unroll=TABLE_UNROLL)
        run_pairs(local, pairs)
        *moments, s = gathered(onehot_of(total, other_vector[...], blocks), pairs)
        weight = coupling_scale * ghost_recv[rows_of(7, 0, total), :]
        for r, moment in enumerate(moments):
            force = weight * (ghost_recv[rows_of(r, 0, total), :] * s - moment)
            for p in range(n):
                sent[p, r] = force[p * padded : (p + 1) * padded]
        exchange(back, sent, got, 1)
        got[me] = sent[me]
        run_pairs(0, local // 2)
        at_home = gathered(onehot_of(blocks, home_vector[...], 0), 0)
        at_other = gathered(onehot_of(blocks, other_vector[...], 0), pairs)
        *moments, s = [a + b for a, b in zip(at_home, at_other)]
        owners = onehot_of(blocks, slots_vector[...], 0)
        settle(recv_sem.at[back], got, 1)
        weight = coupling_scale * state[rows_of(7, 0, blocks), :]
        for r, moment in enumerate(moments):
            place_now = state[rows_of(r, 0, blocks), :]
            force = weight * (place_now * s - moment)
            returned = jnp.concatenate([got[p, r] for p in range(n)], 0)
            high, middle, low = split(returned)
            force = force + (
                nn(owners, high.astype(bf16))
                + nn(owners, middle.astype(bf16))
                + nn(owners, low.astype(bf16))
            )
            speed = state[rows_of(3 + r, 0, blocks), :] + time_step * force
            state[rows_of(3 + r, 0, blocks), :] = speed
            state[rows_of(r, 0, blocks), :] = place_now + time_step * speed
            if step == STEPS - 1:
                force_rows[rows_of(r, 0, blocks), :] = force
        if step < STEPS - 1:

            def stack(b, carry):
                tiles[b] = state[tile_of(b), :]
                return carry

            lax.fori_loop(0, blocks, stack, 0, unroll=UNROLL)

    def finish(b, carry):
        lanes = pl.ds(pl.multiple_of(b * BLOCK, BLOCK), BLOCK)
        tile = state[tile_of(b), :]
        pos_out[:, lanes] = tile[:3]
        vel_out[:, lanes] = tile[3:6]
        force_out[:, lanes] = force_rows[tile_of(b), :][:3]
        return carry

    lax.fori_loop(0, blocks, finish, 0, unroll=UNROLL)
    settle(send_sem.at[0], move_out, 1)
    for step in range(STEPS):
        settle(send_sem.at[1 + 2 * step], ghost_out.at[step], padded * ROWS)
        settle(send_sem.at[2 + 2 * step], force_send.at[step], 1)


def on_device(
    n,
    positions,
    velocities,
    charges,
    solute,
    rest_scale,
    send_slot,
    land_slot,
    ghost_slot,
    pair_home,
    pair_other,
):
    blocks = positions.shape[1] // BLOCK
    ghosts = ghost_slot.shape[1]
    pairs = pair_home.shape[1]
    group = ghosts // n
    padded = -(-group // 8) * 8
    total = n * padded
    other = pair_other
    slots = ghost_slot
    if padded != group:
        ghost = jnp.maximum(pair_other - blocks, 0)
        place = blocks + ghost // group * padded + lax.rem(ghost, group)
        other = jnp.where(pair_other < blocks, pair_other, place)
        extra = ((0, 0), (0, padded - group))
        slots = jnp.pad(ghost_slot.reshape(n, group), extra, constant_values=blocks)
        slots = slots.reshape(1, total)

    vmem = pl.BlockSpec(memory_space=pltpu.VMEM)
    smem = pl.BlockSpec(memory_space=pltpu.SMEM)
    phases = 1 + 2 * STEPS
    everything = blocks + total
    out = jax.ShapeDtypeStruct(positions.shape, f32)
    call = pl.pallas_call(
        functools.partial(kernel, n, blocks, ghosts, padded, pairs),
        out_shape=(out, out, out),
        in_specs=[smem] * 6 + [vmem] * 7,
        out_specs=(vmem, vmem, vmem),
        scratch_shapes=[
            pltpu.VMEM((blocks + n, ROWS, BLOCK), f32),
            pltpu.VMEM((blocks, ROWS, BLOCK), f32),
            pltpu.VMEM((blocks * ROWS, BLOCK), f32),
            pltpu.VMEM((n, ROWS, BLOCK), f32),
            pltpu.VMEM((n, ROWS, BLOCK), f32),
            pltpu.VMEM((STEPS, total * ROWS, BLOCK), f32),
            pltpu.VMEM((STEPS, total * ROWS, BLOCK), f32),
            pltpu.VMEM((STEPS, n, 3, padded, BLOCK), f32),
            pltpu.VMEM((STEPS, n, 3, padded, BLOCK), f32),
            pltpu.VMEM((blocks, BLOCK, DEPTH), bf16),
            pltpu.VMEM((everything, DEPTH, BLOCK), bf16),
            pltpu.VMEM((everything, 16, BLOCK), bf16),
            pltpu.VMEM((everything, ROWS, BLOCK), f32),
            pltpu.VMEM((blocks, BLOCK, BLOCK), f32),
            pltpu.VMEM((2 * pairs * ROWS, BLOCK), f32),
            pltpu.VMEM((blocks * ROWS, BLOCK), f32),
            pltpu.SMEM((blocks,), jnp.int32),
            pltpu.SemaphoreType.DMA((phases,)),
            pltpu.SemaphoreType.DMA((phases,)),
        ],
        compiler_params=pltpu.CompilerParams(collective_id=0, has_side_effects=True),
    )
    return call(
        pair_home,
        other,
        send_slot,
        land_slot,
        ghost_slot,
        rest_scale,
        pair_home,
        other,
        slots,
        positions,
        velocities,
        charges.reshape(blocks, BLOCK),
        solute.reshape(blocks, BLOCK),
    )


def solution(mesh):
    both = ("rep", "dom")
    in_specs = (
        P(None, both),
        P(None, both),
        P(both),
        P(both),
        P("rep"),
        P(both, None),
        P(both, None),
        P(both, None),
        P(both, None),
        P(both, None),
    )
    out_specs = (P(None, both), P(None, both), P(None, both))
    return jax.shard_map(
        functools.partial(on_device, mesh.shape["dom"]),
        mesh=mesh,
        in_specs=in_specs,
        out_specs=out_specs,
        check_vma=False,
    )
```

```python
import functools
import math

import jax
import jax.numpy as jnp
from jax import lax
from jax.experimental import pallas as pl
from jax.experimental.pallas import tpu as pltpu
from jax.sharding import PartitionSpec as P

BLOCK = 128
STEPS = 2
UNROLL = 4
TABLE_UNROLL = 16
PAIR_UNROLL = 64
AHEAD = 6
INPUTS = 14
BEHIND = 3
ROWS = 8
DEPTH = 48

coupling_scale = 0.2
time_step = 0.05
log2e = math.log2(math.e)
f32 = jnp.float32
bf16 = jnp.bfloat16
MESH = pl.DeviceIdType.MESH


def split(value):
    high = value.astype(bf16).astype(f32)
    rest = value - high
    middle = rest.astype(bf16).astype(f32)
    return high, middle, rest - middle


def nn(left, right):
    return lax.dot_general(left, right, (((1,), (0,)), ((), ())), preferred_element_type=f32)


def nt(left, right):
    return lax.dot_general(left, right, (((1,), (1,)), ((), ())), preferred_element_type=f32)


def kernel(
    n,
    blocks,
    ghosts,
    padded,
    pairs,
    *refs,
):
    inputs, moved = refs[:INPUTS], refs[INPUTS]
    fetched, scratch = refs[INPUTS + 1 : 2 * INPUTS + 1], refs[2 * INPUTS + 1 :]
    (
        home_ref,
        other_ref,
        send_ref,
        land_ref,
        slot_ref,
        scale_ref,
        home_vector,
        other_vector,
        slots_vector,
        spread_vector,
        pos_ref,
        vel_ref,
        charge_ref,
        solute_ref,
    ) = fetched
    (
        old,
        state,
        move_out,
        move_in,
        first_out,
        first_in,
        later_out,
        later_in,
        unfolded,
        left_table,
        right_table,
        weighted,
        charge_rows,
        charge_wide,
        results,
        select,
        collect,
        turned,
        source,
        send_sem,
        recv_sem,
        fetch_sem,
    ) = scratch
    me = lax.axis_index("dom")
    group = ghosts // n
    local = pairs - ghosts
    total = n * padded
    row = lax.broadcasted_iota(jnp.int32, (ROWS, BLOCK), 0)

    barrier = pltpu.get_barrier_semaphore()

    def greet(j, carry):
        pl.semaphore_signal(barrier, inc=1, device_id={"dom": lax.rem(me + j, n)}, device_id_type=MESH)
        return carry

    lax.fori_loop(1, n, greet, 0)

    fetches = [
        pltpu.make_async_copy(inputs[i], fetched[i], fetch_sem.at[i]) for i in reversed(range(INPUTS))
    ]
    for fetch in fetches:
        fetch.start()
    for fetch in fetches:
        fetch.wait()

    def partner(i):
        j = n - i
        if n & (n - 1):
            return lax.rem(me + j, n)
        target, bit = 0, 1
        while bit < n:
            target = target + bit * lax.rem(lax.div(me, bit) + lax.div(j, bit), 2)
            bit *= 2
        return target

    root = jnp.sqrt(jnp.broadcast_to(scale_ref[...], (1, BLOCK)))

    def gather_state(b, carry):
        lanes = pl.ds(pl.multiple_of(b * BLOCK, BLOCK), BLOCK)
        weight = jnp.where(solute_ref[pl.ds(b, 1), :] == 1, root, 1.0)
        old[b] = jnp.concatenate(
            [pos_ref[:, lanes], vel_ref[:, lanes], charge_ref[pl.ds(b, 1), :], weight], 0
        )
        return carry

    lax.fori_loop(0, blocks, gather_state, 0, unroll=UNROLL)

    def pack_move(i, carry):
        target = partner(i)
        move_out[target] = old[jnp.minimum(send_ref[0, target], blocks - 1)]
        return carry

    lax.fori_loop(1, n, pack_move, 0)
    pl.semaphore_wait(barrier, n - 1)

    def push(outgoing, incoming, sem):
        def one(i, carry):
            target = partner(i)
            pltpu.make_async_remote_copy(
                src_ref=outgoing.at[target],
                dst_ref=incoming.at[me],
                send_sem=send_sem.at[sem],
                recv_sem=recv_sem.at[sem],
                device_id={"dom": target},
                device_id_type=MESH,
            ).start()
            return carry

        lax.fori_loop(1, n, one, 0)

    def settle(sem, buffer):
        part = buffer.at[pl.ds(0, n - 1)]
        pltpu.make_async_copy(part, part, sem).wait()

    def rows_of(r, start, count):
        return pl.ds(start * ROWS + r, count, stride=ROWS)

    def tile_of(at):
        return pl.ds(pl.multiple_of(at * ROWS, ROWS), ROWS)

    push(move_out, move_in, 0)

    def onehot_of(count, indices, base):
        shape = (count, indices.shape[1])
        hit = lax.broadcasted_iota(jnp.int32, shape, 0) + base == indices
        return jnp.where(hit, 1.0, 0.0).astype(bf16)

    homes = onehot_of(blocks, home_vector[...], 0)
    collect[...] = jnp.concatenate(
        [
            homes,
            onehot_of(blocks, slots_vector[...], 0),
            onehot_of(blocks, other_vector[:, :local], 0),
        ],
        1,
    )
    same = lax.broadcasted_iota(jnp.int32, (total, total), 0)
    same = same == lax.broadcasted_iota(jnp.int32, (total, total), 1)
    same = jnp.where(same, 1.0, 0.0).astype(bf16)
    ghost_pick = nt(same, onehot_of(blocks, spread_vector[...], 0)).astype(bf16)
    home_pick = nt(
        onehot_of(total, other_vector[:, local:], blocks),
        onehot_of(blocks, home_vector[:, local:], 0),
    ).astype(bf16)
    picks_all = jnp.concatenate([ghost_pick, home_pick], 0)
    select[...] = jnp.concatenate([picks_all, picks_all, picks_all], 1)

    def find(s, carry):
        def look(p, best):
            return jnp.where(land_ref[0, p] == s, blocks + p, best)

        source[s] = lax.fori_loop(0, n, look, s, unroll=8)
        return carry

    lax.fori_loop(0, blocks, find, 0, unroll=UNROLL)
    settle(recv_sem.at[0], move_in)

    def unpack(i, carry):
        origin = partner(i)
        old[blocks + origin] = move_in[origin]
        return carry

    lax.fori_loop(1, n, unpack, 0)

    def place(s, carry):
        state[tile_of(s), :] = old[source[s]]
        return carry

    lax.fori_loop(0, blocks, place, 0, unroll=UNROLL)

    def partner_tables(tile, at, first_step):
        squares = jnp.where(row < 3, tile * tile, 0.0)
        norm = (-0.5 * log2e) * jnp.sum(squares, 0, keepdims=True)
        charge = tile[6:7]
        weight = tile[7:8]
        right = jnp.where(
            row < 3, log2e * tile, jnp.where(row == 3, 1.0, jnp.where(row == 4, norm, 0.0))
        )
        high, middle, low = split(right)
        right_table[at] = jnp.concatenate([high, middle, high, middle, low, high], 0).astype(bf16)
        scaled = jnp.where(row < 3, weight * tile, jnp.where(row == 3, weight, 0.0))
        high, middle, low = split(scaled)
        first = jnp.where(row < 4, high, pltpu.roll(low, 4, 0))
        weighted[at] = jnp.concatenate([first, middle], 0).astype(bf16)
        if first_step:
            charge_rows[at] = jnp.broadcast_to(charge, (ROWS, BLOCK))
        return norm, charge

    deep = lax.broadcasted_iota(jnp.int32, (DEPTH, BLOCK), 0)
    picks = jnp.where((deep == 5) | (deep == 21) | (deep == 45), 1.0, 0.0).astype(bf16)

    def home_tables(first_step):
        def one(b, carry):
            tile = state[tile_of(b), :]
            norm, charge = partner_tables(tile, b, first_step)
            left = jnp.where(
                row < 3,
                tile,
                jnp.where(
                    row == 3,
                    norm,
                    jnp.where(row == 4, 1.0, jnp.where(row == 5, charge, 0.0)),
                ),
            )
            high, middle, low = split(left)
            stacked = jnp.concatenate([high, high, middle, middle, high, low], 0)
            upright = stacked.astype(bf16).T
            left_table[b] = upright
            if first_step:
                charge_wide[b] = nn(upright, picks)
            return carry

        lax.fori_loop(0, blocks, one, 0, unroll=TABLE_UNROLL)

    def exponent_of(home, other):
        return nn(left_table[home], right_table[other])

    def couplings(home, other, exponent):
        decay = jnp.exp2(exponent)
        wide = charge_wide[home].reshape(BLOCK // ROWS, ROWS, BLOCK)
        charges = (wide * charge_rows[other][None]).reshape(BLOCK, BLOCK)
        coupling = decay * (charges + decay)
        high = coupling.astype(bf16)
        low = (coupling - high.astype(f32)).astype(bf16)
        return jnp.concatenate([high, low], 1)

    def send_home(other, both, at):
        rows = weighted[other]
        to_home = nt(jnp.concatenate([rows, rows], 1), both)
        results[tile_of(at), :] = to_home[:ROWS] + to_home[ROWS:]

    def send_other(home, both, at):
        to_other = nn(weighted[home], both)
        halves = to_other[:ROWS] + to_other[ROWS:]
        results[tile_of(at), :] = halves[:, :BLOCK] + halves[:, BLOCK:]

    def turn(u, both):
        turned[u, :BLOCK] = both[:, :BLOCK].T
        turned[u, BLOCK:] = both[:, BLOCK:].T

    def send_turned(other, u, at):
        rows = weighted[other]
        to_home = nn(jnp.concatenate([rows, rows], 1), turned[u])
        results[tile_of(at), :] = to_home[:ROWS] + to_home[ROWS:]

    def run_pairs(count, ends, finish, two_sided):
        unroll = math.gcd(count, PAIR_UNROLL)

        def some(i, carry):
            base = i * unroll
            found = [ends(base + u) for u in range(unroll)]
            exponents, coupled = {}, {}
            for u in range(unroll + AHEAD + BEHIND):
                if u < unroll:
                    exponents[u] = exponent_of(*found[u])
                v = u - AHEAD
                if 0 <= v < unroll:
                    coupled[v] = couplings(*found[v], exponents.pop(v))
                    if two_sided:
                        turn(v, coupled[v])
                v = u - AHEAD - BEHIND
                if 0 <= v < unroll:
                    finish(base + v, v, *found[v], coupled.pop(v))
            return carry

        lax.fori_loop(0, count // unroll, some, 0)

    def finish_local(t, u, home, other, both):
        send_other(home, both, pairs + ghosts + t)
        send_turned(other, u, t)

    def run_local():
        run_pairs(local, lambda t: (home_ref[0, t], other_ref[0, t]), finish_local, True)

    def run_ghost():
        run_pairs(
            ghosts,
            lambda t: (home_ref[0, local + t], other_ref[0, local + t]),
            lambda t, u, home, other, both: send_home(other, both, local + t),
            False,
        )

    def run_mirror():
        run_pairs(
            ghosts,
            lambda t: (slot_ref[0, t], blocks + ghosts + t),
            lambda t, u, home, other, both: send_home(other, both, pairs + t),
            False,
        )

    def collected():
        sums = []
        everything = 2 * pairs
        for r in (0, 2):
            values = [
                results[rows_of(r + q, 0, everything), :]
                + results[rows_of(r + q + 4, 0, everything), :]
                for q in range(2)
            ]
            parts = split(jnp.concatenate(values, 1))
            both = sum(nn(collect[...], part.astype(bf16)) for part in reversed(parts))
            sums += [both[:, :BLOCK], both[:, BLOCK:]]
        return sums

    for step in range(STEPS):
        first_step = step == 0
        lines = (0, 1, 2, 6, 7) if first_step else (0, 1, 2)
        outgoing = first_out if first_step else later_out.at[step - 1]
        incoming = first_in if first_step else later_in.at[step - 1]
        planes = [jnp.concatenate(split(state[rows_of(r, 0, blocks), :]), 0) for r in lines]
        for kind in range(2):
            chosen = select[kind * total : (kind + 1) * total, :]
            for at, plane in enumerate(planes):
                taken = nn(chosen, plane.astype(bf16))
                for p in range(n):
                    outgoing[kind, p, at] = taken[p * padded : (p + 1) * padded]
            push(outgoing.at[kind], incoming.at[kind], 1 + 2 * step + kind)
        for kind in range(2):
            incoming[kind, me] = outgoing[kind, me]

        home_tables(first_step)
        run_local()

        for kind in range(2):
            settle(recv_sem.at[1 + 2 * step + kind], incoming.at[kind])
            base = blocks + kind * ghosts

            def remote_tables(p, carry):
                for at, r in enumerate(lines):
                    unfolded[kind, p, pl.ds(r, padded, stride=ROWS), :] = incoming[kind, p, at]
                for k in range(group):
                    tile = unfolded[kind, p, pl.ds(k * ROWS, ROWS), :]
                    partner_tables(tile, base + p * group + k, first_step)
                return carry

            lax.fori_loop(0, n, remote_tables, 0, unroll=2)
            if kind == 0:
                run_ghost()
            else:
                run_mirror()

        *moments, s = collected()
        weight = coupling_scale * state[rows_of(7, 0, blocks), :]
        for r, moment in enumerate(moments):
            place_now = state[rows_of(r, 0, blocks), :]
            force = weight * (place_now * s - moment)
            speed = state[rows_of(3 + r, 0, blocks), :] + time_step * force
            place_now = place_now + time_step * speed
            if step < STEPS - 1:
                state[rows_of(3 + r, 0, blocks), :] = speed
                state[rows_of(r, 0, blocks), :] = place_now
            else:
                moved[r] = place_now
                moved[3 + r] = speed
                moved[6 + r] = force

    settle(send_sem.at[0], move_out)
    for step in range(STEPS):
        outgoing = first_out if step == 0 else later_out.at[step - 1]
        for kind in range(2):
            settle(send_sem.at[1 + 2 * step + kind], outgoing.at[kind])


def unfold(blocks, moved, *outs):
    def one(b, carry):
        lanes = pl.ds(pl.multiple_of(b * BLOCK, BLOCK), BLOCK)
        for i, out in enumerate(outs):
            out[:, lanes] = moved[pl.ds(3 * i * blocks + b, 3, stride=blocks), :]
        return carry

    lax.fori_loop(0, blocks, one, 0, unroll=8)


def on_device(
    n,
    positions,
    velocities,
    charges,
    solute,
    rest_scale,
    send_slot,
    land_slot,
    ghost_slot,
    pair_home,
    pair_other,
):
    blocks = positions.shape[1] // BLOCK
    ghosts = ghost_slot.shape[1]
    pairs = pair_home.shape[1]
    group = ghosts // n
    padded = -(-group // 8) * 8
    total = n * padded
    other = pair_other
    slots = ghost_slot
    if padded != group:
        ghost = jnp.maximum(pair_other - blocks, 0)
        place = blocks + ghost // group * padded + lax.rem(ghost, group)
        other = jnp.where(pair_other < blocks, pair_other, place)
        extra = ((0, 0), (0, padded - group))
        slots = jnp.pad(ghost_slot.reshape(n, group), extra, constant_values=blocks)
        slots = slots.reshape(1, total)

    vmem = pl.BlockSpec(memory_space=pltpu.VMEM)
    hbm = pl.BlockSpec(memory_space=pltpu.HBM)
    phases = 1 + 2 * STEPS
    everything = blocks + 2 * ghosts
    out = jax.ShapeDtypeStruct((9, blocks, BLOCK), f32)
    inputs = (
        pair_home,
        pair_other,
        send_slot,
        land_slot,
        ghost_slot,
        rest_scale.reshape(1, 1),
        pair_home,
        other,
        ghost_slot,
        slots,
        positions,
        velocities,
        charges.reshape(blocks, BLOCK),
        solute.reshape(blocks, BLOCK),
    )
    inputs = tuple(
        value if value.size == 1 else pltpu.with_memory_space_constraint(value, pltpu.HBM)
        for value in inputs
    )
    fetched = [
        (pltpu.SMEM if i < 5 else pltpu.VMEM)(value.shape, value.dtype)
        for i, value in enumerate(inputs)
    ]
    call = pl.pallas_call(
        functools.partial(kernel, n, blocks, ghosts, padded, pairs),
        out_shape=out,
        in_specs=[hbm] * INPUTS,
        out_specs=vmem,
        scratch_shapes=fetched
        + [
            pltpu.VMEM((blocks + n, ROWS, BLOCK), f32),
            pltpu.VMEM((blocks * ROWS, BLOCK), f32),
            pltpu.VMEM((n, ROWS, BLOCK), f32),
            pltpu.VMEM((n, ROWS, BLOCK), f32),
            pltpu.VMEM((2, n, 5, padded, BLOCK), f32),
            pltpu.VMEM((2, n, 5, padded, BLOCK), f32),
            pltpu.VMEM((STEPS - 1, 2, n, 3, padded, BLOCK), f32),
            pltpu.VMEM((STEPS - 1, 2, n, 3, padded, BLOCK), f32),
            pltpu.VMEM((2, n, padded * ROWS, BLOCK), f32),
            pltpu.VMEM((blocks, BLOCK, DEPTH), bf16),
            pltpu.VMEM((everything, DEPTH, BLOCK), bf16),
            pltpu.VMEM((everything, 16, BLOCK), bf16),
            pltpu.VMEM((everything, ROWS, BLOCK), f32),
            pltpu.VMEM((blocks, BLOCK, BLOCK), f32),
            pltpu.VMEM((2 * pairs * ROWS, BLOCK), f32),
            pltpu.VMEM((2 * total, 3 * blocks), bf16),
            pltpu.VMEM((blocks, 2 * pairs), bf16),
            pltpu.VMEM((PAIR_UNROLL, 2 * BLOCK, BLOCK), bf16),
            pltpu.SMEM((blocks,), jnp.int32),
            pltpu.SemaphoreType.DMA((phases,)),
            pltpu.SemaphoreType.DMA((phases,)),
            pltpu.SemaphoreType.DMA((INPUTS,)),
        ],
        compiler_params=pltpu.CompilerParams(
            collective_id=0, has_side_effects=True, vmem_limit_bytes=40 * 2**20
        ),
    )
    moved = call(*inputs)
    out = jax.ShapeDtypeStruct(positions.shape, f32)
    return pl.pallas_call(
        functools.partial(unfold, blocks),
        out_shape=(out, out, out),
        in_specs=[vmem],
        out_specs=(vmem, vmem, vmem),
        compiler_params=pltpu.CompilerParams(vmem_limit_bytes=40 * 2**20),
    )(moved.reshape(9 * blocks, BLOCK))


def solution(mesh):
    both = ("rep", "dom")
    in_specs = (
        P(None, both),
        P(None, both),
        P(both),
        P(both),
        P("rep"),
        P(both, None),
        P(both, None),
        P(both, None),
        P(both, None),
        P(both, None),
    )
    out_specs = (P(None, both), P(None, both), P(None, both))
    return jax.shard_map(
        functools.partial(on_device, mesh.shape["dom"]),
        mesh=mesh,
        in_specs=in_specs,
        out_specs=out_specs,
        check_vma=False,
    )
```

```python
import functools
import math

import jax
import jax.numpy as jnp
from jax import lax
from jax.experimental import pallas as pl
from jax.experimental.pallas import tpu as pltpu
from jax.sharding import PartitionSpec as P

BLOCK = 128
STEPS = 2
UNROLL = 4
TABLE_UNROLL = 16
PAIR_UNROLL = 64
AHEAD = 6
INPUTS = 14
BEHIND = 4
ROWS = 8
DEPTH = 48

coupling_scale = 0.2
time_step = 0.05
log2e = math.log2(math.e)
f32 = jnp.float32
bf16 = jnp.bfloat16
MESH = pl.DeviceIdType.MESH


def split(value):
    high = value.astype(bf16).astype(f32)
    rest = value - high
    middle = rest.astype(bf16).astype(f32)
    return high, middle, rest - middle


def nn(left, right):
    return lax.dot_general(left, right, (((1,), (0,)), ((), ())), preferred_element_type=f32)


def nt(left, right):
    return lax.dot_general(left, right, (((1,), (1,)), ((), ())), preferred_element_type=f32)


def kernel(
    n,
    blocks,
    ghosts,
    padded,
    pairs,
    *refs,
):
    inputs, moved = refs[:INPUTS], refs[INPUTS]
    fetched, scratch = refs[INPUTS + 1 : 2 * INPUTS + 1], refs[2 * INPUTS + 1 :]
    (
        home_ref,
        other_ref,
        send_ref,
        land_ref,
        slot_ref,
        scale_ref,
        home_vector,
        other_vector,
        slots_vector,
        spread_vector,
        pos_ref,
        vel_ref,
        charge_ref,
        solute_ref,
    ) = fetched
    (
        old,
        state,
        move_out,
        move_in,
        first_out,
        first_in,
        later_out,
        later_in,
        unfolded,
        left_table,
        right_table,
        weighted,
        charge_rows,
        charge_wide,
        results,
        select,
        collect,
        turned,
        source,
        send_sem,
        recv_sem,
        fetch_sem,
    ) = scratch
    me = lax.axis_index("dom")
    group = ghosts // n
    local = pairs - ghosts
    total = n * padded
    row = lax.broadcasted_iota(jnp.int32, (ROWS, BLOCK), 0)

    barrier = pltpu.get_barrier_semaphore()

    def greet(j, carry):
        pl.semaphore_signal(barrier, inc=1, device_id={"dom": lax.rem(me + j, n)}, device_id_type=MESH)
        return carry

    lax.fori_loop(1, n, greet, 0)

    fetches = [
        pltpu.make_async_copy(inputs[i], fetched[i], fetch_sem.at[i]) for i in reversed(range(INPUTS))
    ]
    for fetch in fetches:
        fetch.start()
    for fetch in fetches:
        fetch.wait()

    def partner(i):
        j = n - i
        if n & (n - 1):
            return lax.rem(me + j, n)
        target, bit = 0, 1
        while bit < n:
            target = target + bit * lax.rem(lax.div(me, bit) + lax.div(j, bit), 2)
            bit *= 2
        return target

    root = jnp.sqrt(jnp.broadcast_to(scale_ref[...], (1, BLOCK)))

    def gather_state(b, carry):
        lanes = pl.ds(pl.multiple_of(b * BLOCK, BLOCK), BLOCK)
        weight = jnp.where(solute_ref[pl.ds(b, 1), :] == 1, root, 1.0)
        old[b] = jnp.concatenate(
            [pos_ref[:, lanes], vel_ref[:, lanes], charge_ref[pl.ds(b, 1), :], weight], 0
        )
        return carry

    lax.fori_loop(0, blocks, gather_state, 0, unroll=UNROLL)

    def pack_move(i, carry):
        target = partner(i)
        move_out[target] = old[jnp.minimum(send_ref[0, target], blocks - 1)]
        return carry

    lax.fori_loop(1, n, pack_move, 0)
    pl.semaphore_wait(barrier, n - 1)

    def push(outgoing, incoming, sem):
        def one(i, carry):
            target = partner(i)
            pltpu.make_async_remote_copy(
                src_ref=outgoing.at[target],
                dst_ref=incoming.at[me],
                send_sem=send_sem.at[sem],
                recv_sem=recv_sem.at[sem],
                device_id={"dom": target},
                device_id_type=MESH,
            ).start()
            return carry

        lax.fori_loop(1, n, one, 0)

    def settle(sem, buffer):
        part = buffer.at[pl.ds(0, n - 1)]
        pltpu.make_async_copy(part, part, sem).wait()

    def rows_of(r, start, count):
        return pl.ds(start * ROWS + r, count, stride=ROWS)

    def tile_of(at):
        return pl.ds(pl.multiple_of(at * ROWS, ROWS), ROWS)

    push(move_out, move_in, 0)

    def onehot_of(count, indices, base):
        shape = (count, indices.shape[1])
        hit = lax.broadcasted_iota(jnp.int32, shape, 0) + base == indices
        return jnp.where(hit, 1.0, 0.0).astype(bf16)

    homes = onehot_of(blocks, home_vector[...], 0)
    collect[...] = jnp.concatenate(
        [
            homes[:, :local],
            onehot_of(blocks, other_vector[:, :local], 0),
            homes[:, local:],
            onehot_of(blocks, slots_vector[...], 0),
        ],
        1,
    )
    same = lax.broadcasted_iota(jnp.int32, (total, total), 0)
    same = same == lax.broadcasted_iota(jnp.int32, (total, total), 1)
    same = jnp.where(same, 1.0, 0.0).astype(bf16)
    ghost_pick = nt(same, onehot_of(blocks, spread_vector[...], 0)).astype(bf16)
    home_pick = nt(
        onehot_of(total, other_vector[:, local:], blocks),
        onehot_of(blocks, home_vector[:, local:], 0),
    ).astype(bf16)
    picks_all = jnp.concatenate([ghost_pick, home_pick], 0)
    select[...] = jnp.concatenate([picks_all, picks_all, picks_all], 1)

    def find(s, carry):
        def look(p, best):
            return jnp.where(land_ref[0, p] == s, blocks + p, best)

        source[s] = lax.fori_loop(0, n, look, s, unroll=8)
        return carry

    lax.fori_loop(0, blocks, find, 0, unroll=UNROLL)
    settle(recv_sem.at[0], move_in)

    def unpack(i, carry):
        origin = partner(i)
        old[blocks + origin] = move_in[origin]
        return carry

    lax.fori_loop(1, n, unpack, 0)

    def place(s, carry):
        state[tile_of(s), :] = old[source[s]]
        return carry

    lax.fori_loop(0, blocks, place, 0, unroll=UNROLL)

    def partner_tables(tile, at, first_step):
        squares = jnp.where(row < 3, tile * tile, 0.0)
        norm = (-0.5 * log2e) * jnp.sum(squares, 0, keepdims=True)
        charge = tile[6:7]
        weight = tile[7:8]
        right = jnp.where(
            row < 3, log2e * tile, jnp.where(row == 3, 1.0, jnp.where(row == 4, norm, 0.0))
        )
        high, middle, low = split(right)
        right_table[at] = jnp.concatenate([high, middle, high, middle, low, high], 0).astype(bf16)
        scaled = jnp.where(row < 3, weight * tile, jnp.where(row == 3, weight, 0.0))
        high, middle, low = split(scaled)
        first = jnp.where(row < 4, high, pltpu.roll(low, 4, 0))
        weighted[at] = jnp.concatenate([first, middle], 0).astype(bf16)
        if first_step:
            charge_rows[at] = jnp.broadcast_to(charge, (ROWS, BLOCK))
        return norm, charge

    deep = lax.broadcasted_iota(jnp.int32, (DEPTH, BLOCK), 0)
    picks = jnp.where((deep == 5) | (deep == 21) | (deep == 45), 1.0, 0.0).astype(bf16)

    def home_tables(first_step):
        def one(b, carry):
            tile = state[tile_of(b), :]
            norm, charge = partner_tables(tile, b, first_step)
            left = jnp.where(
                row < 3,
                tile,
                jnp.where(
                    row == 3,
                    norm,
                    jnp.where(row == 4, 1.0, jnp.where(row == 5, charge, 0.0)),
                ),
            )
            high, middle, low = split(left)
            stacked = jnp.concatenate([high, high, middle, middle, high, low], 0)
            upright = stacked.astype(bf16).T
            left_table[b] = upright
            if first_step:
                charge_wide[b] = nn(upright, picks)
            return carry

        lax.fori_loop(0, blocks, one, 0, unroll=TABLE_UNROLL)

    def exponent_of(home, other):
        return nn(left_table[home], right_table[other])

    def couplings(home, other, exponent):
        decay = jnp.exp2(exponent)
        wide = charge_wide[home].reshape(BLOCK // ROWS, ROWS, BLOCK)
        charges = (wide * charge_rows[other][None]).reshape(BLOCK, BLOCK)
        coupling = decay * (charges + decay)
        high = coupling.astype(bf16)
        low = (coupling - high.astype(f32)).astype(bf16)
        return jnp.concatenate([high, low], 1)

    def send_home(other, both, at):
        rows = weighted[other]
        to_home = nt(jnp.concatenate([rows, rows], 1), both)
        results[tile_of(at), :] = to_home[:ROWS] + to_home[ROWS:]

    def send_other(home, both, at):
        to_other = nn(weighted[home], both)
        halves = to_other[:ROWS] + to_other[ROWS:]
        results[tile_of(at), :] = halves[:, :BLOCK] + halves[:, BLOCK:]

    def turn(u, both):
        turned[u, :BLOCK] = both[:, :BLOCK].T
        turned[u, BLOCK:] = both[:, BLOCK:].T

    def send_turned(other, u, at):
        rows = weighted[other]
        to_home = nn(jnp.concatenate([rows, rows], 1), turned[u])
        results[tile_of(at), :] = to_home[:ROWS] + to_home[ROWS:]

    def run_pairs(count, ends, finish, two_sided):
        unroll = math.gcd(count, PAIR_UNROLL)

        def some(i, carry):
            base = i * unroll
            found = [ends(base + u) for u in range(unroll)]
            exponents, coupled = {}, {}
            for u in range(unroll + AHEAD + BEHIND):
                if u < unroll:
                    exponents[u] = exponent_of(*found[u])
                v = u - AHEAD
                if 0 <= v < unroll:
                    coupled[v] = couplings(*found[v], exponents.pop(v))
                    if two_sided:
                        turn(v, coupled[v])
                v = u - AHEAD - BEHIND
                if 0 <= v < unroll:
                    finish(base + v, v, *found[v], coupled.pop(v))
            return carry

        lax.fori_loop(0, count // unroll, some, 0)

    def finish_local(t, u, home, other, both):
        send_other(home, both, local + t)
        send_turned(other, u, t)

    def run_local():
        run_pairs(local, lambda t: (home_ref[0, t], other_ref[0, t]), finish_local, True)

    def run_ghost():
        run_pairs(
            ghosts,
            lambda t: (home_ref[0, local + t], other_ref[0, local + t]),
            lambda t, u, home, other, both: send_home(other, both, 2 * local + t),
            False,
        )

    def run_mirror():
        run_pairs(
            ghosts,
            lambda t: (slot_ref[0, t], blocks + ghosts + t),
            lambda t, u, home, other, both: send_home(other, both, 2 * local + ghosts + t),
            False,
        )

    def collected(start, count):
        sums = []
        chosen = collect[:, start : start + count]
        for r in (0, 2):
            values = [
                results[rows_of(r + q, start, count), :]
                + results[rows_of(r + q + 4, start, count), :]
                for q in range(2)
            ]
            parts = split(jnp.concatenate(values, 1))
            both = sum(nn(chosen, part.astype(bf16)) for part in reversed(parts))
            sums += [both[:, :BLOCK], both[:, BLOCK:]]
        return sums

    for step in range(STEPS):
        first_step = step == 0
        lines = (0, 1, 2, 6, 7) if first_step else (0, 1, 2)
        outgoing = first_out if first_step else later_out.at[step - 1]
        incoming = first_in if first_step else later_in.at[step - 1]
        planes = [jnp.concatenate(split(state[rows_of(r, 0, blocks), :]), 0) for r in lines]
        for kind in range(2):
            chosen = select[kind * total : (kind + 1) * total, :]
            for at, plane in enumerate(planes):
                taken = nn(chosen, plane.astype(bf16))
                for p in range(n):
                    outgoing[kind, p, at] = taken[p * padded : (p + 1) * padded]
            push(outgoing.at[kind], incoming.at[kind], 1 + 2 * step + kind)
        for kind in range(2):
            incoming[kind, me] = outgoing[kind, me]

        home_tables(first_step)
        run_local()
        early = collected(0, 2 * local)

        for kind in range(2):
            settle(recv_sem.at[1 + 2 * step + kind], incoming.at[kind])
            base = blocks + kind * ghosts

            def remote_tables(p, carry):
                for at, r in enumerate(lines):
                    unfolded[kind, p, pl.ds(r, padded, stride=ROWS), :] = incoming[kind, p, at]
                for k in range(group):
                    tile = unfolded[kind, p, pl.ds(k * ROWS, ROWS), :]
                    partner_tables(tile, base + p * group + k, first_step)
                return carry

            lax.fori_loop(0, n, remote_tables, 0, unroll=2)
            if kind == 0:
                run_ghost()
            else:
                run_mirror()

        late = collected(2 * local, 2 * ghosts)
        *moments, s = [a + b for a, b in zip(early, late)]
        weight = coupling_scale * state[rows_of(7, 0, blocks), :]
        for r, moment in enumerate(moments):
            place_now = state[rows_of(r, 0, blocks), :]
            force = weight * (place_now * s - moment)
            speed = state[rows_of(3 + r, 0, blocks), :] + time_step * force
            place_now = place_now + time_step * speed
            if step < STEPS - 1:
                state[rows_of(3 + r, 0, blocks), :] = speed
                state[rows_of(r, 0, blocks), :] = place_now
            else:
                moved[r] = place_now
                moved[3 + r] = speed
                moved[6 + r] = force

    settle(send_sem.at[0], move_out)
    for step in range(STEPS):
        outgoing = first_out if step == 0 else later_out.at[step - 1]
        for kind in range(2):
            settle(send_sem.at[1 + 2 * step + kind], outgoing.at[kind])


def unfold(blocks, moved, *outs):
    def one(b, carry):
        lanes = pl.ds(pl.multiple_of(b * BLOCK, BLOCK), BLOCK)
        for i, out in enumerate(outs):
            out[:, lanes] = moved[pl.ds(3 * i * blocks + b, 3, stride=blocks), :]
        return carry

    lax.fori_loop(0, blocks, one, 0, unroll=8)


def on_device(
    n,
    positions,
    velocities,
    charges,
    solute,
    rest_scale,
    send_slot,
    land_slot,
    ghost_slot,
    pair_home,
    pair_other,
):
    blocks = positions.shape[1] // BLOCK
    ghosts = ghost_slot.shape[1]
    pairs = pair_home.shape[1]
    group = ghosts // n
    padded = -(-group // 8) * 8
    total = n * padded
    other = pair_other
    slots = ghost_slot
    if padded != group:
        ghost = jnp.maximum(pair_other - blocks, 0)
        place = blocks + ghost // group * padded + lax.rem(ghost, group)
        other = jnp.where(pair_other < blocks, pair_other, place)
        extra = ((0, 0), (0, padded - group))
        slots = jnp.pad(ghost_slot.reshape(n, group), extra, constant_values=blocks)
        slots = slots.reshape(1, total)

    vmem = pl.BlockSpec(memory_space=pltpu.VMEM)
    hbm = pl.BlockSpec(memory_space=pltpu.HBM)
    phases = 1 + 2 * STEPS
    everything = blocks + 2 * ghosts
    out = jax.ShapeDtypeStruct((9, blocks, BLOCK), f32)
    inputs = (
        pair_home,
        pair_other,
        send_slot,
        land_slot,
        ghost_slot,
        rest_scale.reshape(1, 1),
        pair_home,
        other,
        ghost_slot,
        slots,
        positions,
        velocities,
        charges.reshape(blocks, BLOCK),
        solute.reshape(blocks, BLOCK),
    )
    inputs = tuple(
        value if value.size == 1 else pltpu.with_memory_space_constraint(value, pltpu.HBM)
        for value in inputs
    )
    fetched = [
        (pltpu.SMEM if i < 5 else pltpu.VMEM)(value.shape, value.dtype)
        for i, value in enumerate(inputs)
    ]
    call = pl.pallas_call(
        functools.partial(kernel, n, blocks, ghosts, padded, pairs),
        out_shape=out,
        in_specs=[hbm] * INPUTS,
        out_specs=vmem,
        scratch_shapes=fetched
        + [
            pltpu.VMEM((blocks + n, ROWS, BLOCK), f32),
            pltpu.VMEM((blocks * ROWS, BLOCK), f32),
            pltpu.VMEM((n, ROWS, BLOCK), f32),
            pltpu.VMEM((n, ROWS, BLOCK), f32),
            pltpu.VMEM((2, n, 5, padded, BLOCK), f32),
            pltpu.VMEM((2, n, 5, padded, BLOCK), f32),
            pltpu.VMEM((STEPS - 1, 2, n, 3, padded, BLOCK), f32),
            pltpu.VMEM((STEPS - 1, 2, n, 3, padded, BLOCK), f32),
            pltpu.VMEM((2, n, padded * ROWS, BLOCK), f32),
            pltpu.VMEM((blocks, BLOCK, DEPTH), bf16),
            pltpu.VMEM((everything, DEPTH, BLOCK), bf16),
            pltpu.VMEM((everything, 16, BLOCK), bf16),
            pltpu.VMEM((everything, ROWS, BLOCK), f32),
            pltpu.VMEM((blocks, BLOCK, BLOCK), f32),
            pltpu.VMEM((2 * pairs * ROWS, BLOCK), f32),
            pltpu.VMEM((2 * total, 3 * blocks), bf16),
            pltpu.VMEM((blocks, 2 * pairs), bf16),
            pltpu.VMEM((PAIR_UNROLL, 2 * BLOCK, BLOCK), bf16),
            pltpu.SMEM((blocks,), jnp.int32),
            pltpu.SemaphoreType.DMA((phases,)),
            pltpu.SemaphoreType.DMA((phases,)),
            pltpu.SemaphoreType.DMA((INPUTS,)),
        ],
        compiler_params=pltpu.CompilerParams(
            collective_id=0, has_side_effects=True, vmem_limit_bytes=40 * 2**20
        ),
    )
    moved = call(*inputs)
    out = jax.ShapeDtypeStruct(positions.shape, f32)
    return pl.pallas_call(
        functools.partial(unfold, blocks),
        out_shape=(out, out, out),
        in_specs=[vmem],
        out_specs=(vmem, vmem, vmem),
        compiler_params=pltpu.CompilerParams(vmem_limit_bytes=40 * 2**20),
    )(moved.reshape(9 * blocks, BLOCK))


def solution(mesh):
    both = ("rep", "dom")
    in_specs = (
        P(None, both),
        P(None, both),
        P(both),
        P(both),
        P("rep"),
        P(both, None),
        P(both, None),
        P(both, None),
        P(both, None),
        P(both, None),
    )
    out_specs = (P(None, both), P(None, both), P(None, both))
    return jax.shard_map(
        functools.partial(on_device, mesh.shape["dom"]),
        mesh=mesh,
        in_specs=in_specs,
        out_specs=out_specs,
        check_vma=False,
    )
```

```python
import functools
import math

import jax
import jax.numpy as jnp
from jax import lax
from jax.experimental import pallas as pl
from jax.experimental.pallas import tpu as pltpu
from jax.sharding import PartitionSpec as P

BLOCK = 128
STEPS = 2
UNROLL = 4
TABLE_UNROLL = 32
PAIR_UNROLL = 64
AHEAD = 6
INPUTS = 14
BEHIND = 4
ROWS = 8
DEPTH = 48

coupling_scale = 0.2
time_step = 0.05
log2e = math.log2(math.e)
f32 = jnp.float32
bf16 = jnp.bfloat16
MESH = pl.DeviceIdType.MESH


def split(value):
    high = value.astype(bf16).astype(f32)
    rest = value - high
    middle = rest.astype(bf16).astype(f32)
    return high, middle, rest - middle


def nn(left, right):
    return lax.dot_general(left, right, (((1,), (0,)), ((), ())), preferred_element_type=f32)


def nt(left, right):
    return lax.dot_general(left, right, (((1,), (1,)), ((), ())), preferred_element_type=f32)


def kernel(
    n,
    blocks,
    ghosts,
    padded,
    pairs,
    *refs,
):
    inputs, moved = refs[:INPUTS], refs[INPUTS]
    fetched, scratch = refs[INPUTS + 1 : 2 * INPUTS + 1], refs[2 * INPUTS + 1 :]
    (
        home_ref,
        other_ref,
        send_ref,
        land_ref,
        slot_ref,
        scale_ref,
        home_vector,
        other_vector,
        slots_vector,
        spread_vector,
        pos_ref,
        vel_ref,
        charge_ref,
        solute_ref,
    ) = fetched
    (
        old,
        state,
        move_out,
        move_in,
        first_out,
        first_in,
        later_out,
        later_in,
        unfolded,
        left_table,
        right_table,
        weighted,
        charge_rows,
        charge_wide,
        results,
        select,
        collect,
        turned,
        source,
        send_sem,
        recv_sem,
        fetch_sem,
    ) = scratch
    me = lax.axis_index("dom")
    group = ghosts // n
    local = pairs - ghosts
    total = n * padded
    row = lax.broadcasted_iota(jnp.int32, (ROWS, BLOCK), 0)

    barrier = pltpu.get_barrier_semaphore()

    def greet(j, carry):
        pl.semaphore_signal(barrier, inc=1, device_id={"dom": lax.rem(me + j, n)}, device_id_type=MESH)
        return carry

    lax.fori_loop(1, n, greet, 0)

    fetches = [
        pltpu.make_async_copy(inputs[i], fetched[i], fetch_sem.at[i]) for i in reversed(range(INPUTS))
    ]
    for fetch in fetches:
        fetch.start()
    for fetch in fetches:
        fetch.wait()

    def partner(i):
        j = n - i
        if n & (n - 1):
            return lax.rem(me + j, n)
        target, bit = 0, 1
        while bit < n:
            target = target + bit * lax.rem(lax.div(me, bit) + lax.div(j, bit), 2)
            bit *= 2
        return target

    root = jnp.sqrt(jnp.broadcast_to(scale_ref[...], (1, BLOCK)))

    def gather_state(b, carry):
        lanes = pl.ds(pl.multiple_of(b * BLOCK, BLOCK), BLOCK)
        weight = jnp.where(solute_ref[pl.ds(b, 1), :] == 1, root, 1.0)
        old[b] = jnp.concatenate(
            [pos_ref[:, lanes], vel_ref[:, lanes], charge_ref[pl.ds(b, 1), :], weight], 0
        )
        return carry

    lax.fori_loop(0, blocks, gather_state, 0, unroll=UNROLL)

    def pack_move(i, carry):
        target = partner(i)
        move_out[target] = old[jnp.minimum(send_ref[0, target], blocks - 1)]
        return carry

    lax.fori_loop(1, n, pack_move, 0)
    pl.semaphore_wait(barrier, n - 1)

    def push(outgoing, incoming, sem):
        def one(i, carry):
            target = partner(i)
            pltpu.make_async_remote_copy(
                src_ref=outgoing.at[target],
                dst_ref=incoming.at[me],
                send_sem=send_sem.at[sem],
                recv_sem=recv_sem.at[sem],
                device_id={"dom": target},
                device_id_type=MESH,
            ).start()
            return carry

        lax.fori_loop(1, n, one, 0)

    def settle(sem, buffer):
        part = buffer.at[pl.ds(0, n - 1)]
        pltpu.make_async_copy(part, part, sem).wait()

    def rows_of(r, start, count):
        return pl.ds(start * ROWS + r, count, stride=ROWS)

    def tile_of(at):
        return pl.ds(pl.multiple_of(at * ROWS, ROWS), ROWS)

    push(move_out, move_in, 0)

    def onehot_of(count, indices, base):
        shape = (count, indices.shape[1])
        hit = lax.broadcasted_iota(jnp.int32, shape, 0) + base == indices
        return jnp.where(hit, 1.0, 0.0).astype(bf16)

    homes = onehot_of(blocks, home_vector[...], 0)
    collect[...] = jnp.concatenate(
        [
            homes[:, :local],
            onehot_of(blocks, other_vector[:, :local], 0),
            homes[:, local:],
            onehot_of(blocks, slots_vector[...], 0),
        ],
        1,
    )
    same = lax.broadcasted_iota(jnp.int32, (total, total), 0)
    same = same == lax.broadcasted_iota(jnp.int32, (total, total), 1)
    same = jnp.where(same, 1.0, 0.0).astype(bf16)
    ghost_pick = nt(same, onehot_of(blocks, spread_vector[...], 0)).astype(bf16)
    home_pick = nt(
        onehot_of(total, other_vector[:, local:], blocks),
        onehot_of(blocks, home_vector[:, local:], 0),
    ).astype(bf16)
    picks_all = jnp.concatenate([ghost_pick, home_pick], 0)
    select[...] = jnp.concatenate([picks_all, picks_all, picks_all], 1)

    def find(s, carry):
        def look(p, best):
            return jnp.where(land_ref[0, p] == s, blocks + p, best)

        source[s] = lax.fori_loop(0, n, look, s, unroll=8)
        return carry

    lax.fori_loop(0, blocks, find, 0, unroll=UNROLL)
    settle(recv_sem.at[0], move_in)

    def unpack(i, carry):
        origin = partner(i)
        old[blocks + origin] = move_in[origin]
        return carry

    lax.fori_loop(1, n, unpack, 0)

    def place(s, carry):
        state[tile_of(s), :] = old[source[s]]
        return carry

    lax.fori_loop(0, blocks, place, 0, unroll=UNROLL)

    def partner_tables(tile, at, first_step):
        squares = jnp.where(row < 3, tile * tile, 0.0)
        norm = (-0.5 * log2e) * jnp.sum(squares, 0, keepdims=True)
        charge = tile[6:7]
        weight = tile[7:8]
        right = jnp.where(
            row < 3, log2e * tile, jnp.where(row == 3, 1.0, jnp.where(row == 4, norm, 0.0))
        )
        high, middle, low = split(right)
        right_table[at] = jnp.concatenate([high, middle, high, middle, low, high], 0).astype(bf16)
        scaled = jnp.where(row < 3, weight * tile, jnp.where(row == 3, weight, 0.0))
        high, middle, low = split(scaled)
        first = jnp.where(row < 4, high, pltpu.roll(low, 4, 0))
        weighted[at] = jnp.concatenate([first, middle], 0).astype(bf16)
        if first_step:
            charge_rows[at] = jnp.broadcast_to(charge, (ROWS, BLOCK))
        return norm, charge

    deep = lax.broadcasted_iota(jnp.int32, (DEPTH, BLOCK), 0)
    picks = jnp.where((deep == 5) | (deep == 21) | (deep == 45), 1.0, 0.0).astype(bf16)

    def home_tables(first_step):
        def one(b, carry):
            tile = state[tile_of(b), :]
            norm, charge = partner_tables(tile, b, first_step)
            left = jnp.where(
                row < 3,
                tile,
                jnp.where(
                    row == 3,
                    norm,
                    jnp.where(row == 4, 1.0, jnp.where(row == 5, charge, 0.0)),
                ),
            )
            high, middle, low = split(left)
            stacked = jnp.concatenate([high, high, middle, middle, high, low], 0)
            upright = stacked.astype(bf16).T
            left_table[b] = upright
            if first_step:
                charge_wide[b] = nn(upright, picks)
            return carry

        lax.fori_loop(0, blocks, one, 0, unroll=TABLE_UNROLL)

    def exponent_of(home, other):
        return nn(left_table[home], right_table[other])

    def couplings(home, other, exponent):
        decay = jnp.exp2(exponent)
        wide = charge_wide[home].reshape(BLOCK // ROWS, ROWS, BLOCK)
        charges = (wide * charge_rows[other][None]).reshape(BLOCK, BLOCK)
        coupling = decay * (charges + decay)
        high = coupling.astype(bf16)
        low = (coupling - high.astype(f32)).astype(bf16)
        return jnp.concatenate([high, low], 1)

    def send_home(other, both, at):
        rows = weighted[other]
        to_home = nt(jnp.concatenate([rows, rows], 1), both)
        results[tile_of(at), :] = to_home[:ROWS] + to_home[ROWS:]

    def send_other(home, both, at):
        to_other = nn(weighted[home], both)
        halves = to_other[:ROWS] + to_other[ROWS:]
        results[tile_of(at), :] = halves[:, :BLOCK] + halves[:, BLOCK:]

    def turn(u, both):
        turned[u, :BLOCK] = both[:, :BLOCK].T
        turned[u, BLOCK:] = both[:, BLOCK:].T

    def send_turned(other, u, at):
        rows = weighted[other]
        to_home = nn(jnp.concatenate([rows, rows], 1), turned[u])
        results[tile_of(at), :] = to_home[:ROWS] + to_home[ROWS:]

    def run_pairs(count, ends, finish, two_sided):
        unroll = math.gcd(count, PAIR_UNROLL)

        def some(i, carry):
            base = i * unroll
            found = [ends(base + u) for u in range(unroll)]
            exponents, coupled = {}, {}
            behind = BEHIND if two_sided else 2
            for u in range(unroll + AHEAD + behind):
                if u < unroll:
                    exponents[u] = exponent_of(*found[u])
                v = u - AHEAD
                if 0 <= v < unroll:
                    coupled[v] = couplings(*found[v], exponents.pop(v))
                    if two_sided:
                        turn(v, coupled[v])
                v = u - AHEAD - behind
                if 0 <= v < unroll:
                    finish(base + v, v, *found[v], coupled.pop(v))
            return carry

        lax.fori_loop(0, count // unroll, some, 0)

    def finish_local(t, u, home, other, both):
        send_other(home, both, local + t)
        send_turned(other, u, t)

    def run_local():
        run_pairs(local, lambda t: (home_ref[0, t], other_ref[0, t]), finish_local, True)

    def run_ghost():
        run_pairs(
            ghosts,
            lambda t: (home_ref[0, local + t], other_ref[0, local + t]),
            lambda t, u, home, other, both: send_home(other, both, 2 * local + t),
            False,
        )

    def run_mirror():
        run_pairs(
            ghosts,
            lambda t: (slot_ref[0, t], blocks + ghosts + t),
            lambda t, u, home, other, both: send_home(other, both, 2 * local + ghosts + t),
            False,
        )

    def collected(start, count):
        sums = []
        chosen = collect[:, start : start + count]
        for r in (0, 2):
            values = [
                results[rows_of(r + q, start, count), :]
                + results[rows_of(r + q + 4, start, count), :]
                for q in range(2)
            ]
            parts = split(jnp.concatenate(values, 1))
            both = sum(nn(chosen, part.astype(bf16)) for part in reversed(parts))
            sums += [both[:, :BLOCK], both[:, BLOCK:]]
        return sums

    for step in range(STEPS):
        first_step = step == 0
        lines = (0, 1, 2, 6, 7) if first_step else (0, 1, 2)
        outgoing = first_out if first_step else later_out.at[step - 1]
        incoming = first_in if first_step else later_in.at[step - 1]
        planes = [jnp.concatenate(split(state[rows_of(r, 0, blocks), :]), 0) for r in lines]
        for kind in range(2):
            chosen = select[kind * total : (kind + 1) * total, :]
            for at, plane in enumerate(planes):
                taken = nn(chosen, plane.astype(bf16))
                for p in range(n):
                    outgoing[kind, p, at] = taken[p * padded : (p + 1) * padded]
            push(outgoing.at[kind], incoming.at[kind], 1 + 2 * step + kind)
        for kind in range(2):
            incoming[kind, me] = outgoing[kind, me]

        home_tables(first_step)
        run_local()
        early = collected(0, 2 * local)

        for kind in range(2):
            settle(recv_sem.at[1 + 2 * step + kind], incoming.at[kind])
            base = blocks + kind * ghosts

            def remote_tables(p, carry):
                for at, r in enumerate(lines):
                    unfolded[kind, p, pl.ds(r, padded, stride=ROWS), :] = incoming[kind, p, at]
                for k in range(group):
                    tile = unfolded[kind, p, pl.ds(k * ROWS, ROWS), :]
                    partner_tables(tile, base + p * group + k, first_step)
                return carry

            lax.fori_loop(0, n, remote_tables, 0, unroll=2)
            if kind == 0:
                run_ghost()
            else:
                run_mirror()

        late = collected(2 * local, 2 * ghosts)
        *moments, s = [a + b for a, b in zip(early, late)]
        weight = coupling_scale * state[rows_of(7, 0, blocks), :]
        for r, moment in enumerate(moments):
            place_now = state[rows_of(r, 0, blocks), :]
            force = weight * (place_now * s - moment)
            speed = state[rows_of(3 + r, 0, blocks), :] + time_step * force
            place_now = place_now + time_step * speed
            if step < STEPS - 1:
                state[rows_of(3 + r, 0, blocks), :] = speed
                state[rows_of(r, 0, blocks), :] = place_now
            else:
                moved[r] = place_now
                moved[3 + r] = speed
                moved[6 + r] = force

    settle(send_sem.at[0], move_out)
    for step in range(STEPS):
        outgoing = first_out if step == 0 else later_out.at[step - 1]
        for kind in range(2):
            settle(send_sem.at[1 + 2 * step + kind], outgoing.at[kind])


def unfold(blocks, moved, *outs):
    def one(b, carry):
        lanes = pl.ds(pl.multiple_of(b * BLOCK, BLOCK), BLOCK)
        for i, out in enumerate(outs):
            out[:, lanes] = moved[pl.ds(3 * i * blocks + b, 3, stride=blocks), :]
        return carry

    lax.fori_loop(0, blocks, one, 0, unroll=8)


def on_device(
    n,
    positions,
    velocities,
    charges,
    solute,
    rest_scale,
    send_slot,
    land_slot,
    ghost_slot,
    pair_home,
    pair_other,
):
    blocks = positions.shape[1] // BLOCK
    ghosts = ghost_slot.shape[1]
    pairs = pair_home.shape[1]
    group = ghosts // n
    padded = -(-group // 8) * 8
    total = n * padded
    other = pair_other
    slots = ghost_slot
    if padded != group:
        ghost = jnp.maximum(pair_other - blocks, 0)
        place = blocks + ghost // group * padded + lax.rem(ghost, group)
        other = jnp.where(pair_other < blocks, pair_other, place)
        extra = ((0, 0), (0, padded - group))
        slots = jnp.pad(ghost_slot.reshape(n, group), extra, constant_values=blocks)
        slots = slots.reshape(1, total)

    vmem = pl.BlockSpec(memory_space=pltpu.VMEM)
    hbm = pl.BlockSpec(memory_space=pltpu.HBM)
    phases = 1 + 2 * STEPS
    everything = blocks + 2 * ghosts
    out = jax.ShapeDtypeStruct((9, blocks, BLOCK), f32)
    inputs = (
        pair_home,
        pair_other,
        send_slot,
        land_slot,
        ghost_slot,
        rest_scale.reshape(1, 1),
        pair_home,
        other,
        ghost_slot,
        slots,
        positions,
        velocities,
        charges.reshape(blocks, BLOCK),
        solute.reshape(blocks, BLOCK),
    )
    inputs = tuple(
        value if value.size == 1 else pltpu.with_memory_space_constraint(value, pltpu.HBM)
        for value in inputs
    )
    fetched = [
        (pltpu.SMEM if i < 5 else pltpu.VMEM)(value.shape, value.dtype)
        for i, value in enumerate(inputs)
    ]
    call = pl.pallas_call(
        functools.partial(kernel, n, blocks, ghosts, padded, pairs),
        out_shape=out,
        in_specs=[hbm] * INPUTS,
        out_specs=vmem,
        scratch_shapes=fetched
        + [
            pltpu.VMEM((blocks + n, ROWS, BLOCK), f32),
            pltpu.VMEM((blocks * ROWS, BLOCK), f32),
            pltpu.VMEM((n, ROWS, BLOCK), f32),
            pltpu.VMEM((n, ROWS, BLOCK), f32),
            pltpu.VMEM((2, n, 5, padded, BLOCK), f32),
            pltpu.VMEM((2, n, 5, padded, BLOCK), f32),
            pltpu.VMEM((STEPS - 1, 2, n, 3, padded, BLOCK), f32),
            pltpu.VMEM((STEPS - 1, 2, n, 3, padded, BLOCK), f32),
            pltpu.VMEM((2, n, padded * ROWS, BLOCK), f32),
            pltpu.VMEM((blocks, BLOCK, DEPTH), bf16),
            pltpu.VMEM((everything, DEPTH, BLOCK), bf16),
            pltpu.VMEM((everything, 16, BLOCK), bf16),
            pltpu.VMEM((everything, ROWS, BLOCK), f32),
            pltpu.VMEM((blocks, BLOCK, BLOCK), f32),
            pltpu.VMEM((2 * pairs * ROWS, BLOCK), f32),
            pltpu.VMEM((2 * total, 3 * blocks), bf16),
            pltpu.VMEM((blocks, 2 * pairs), bf16),
            pltpu.VMEM((PAIR_UNROLL, 2 * BLOCK, BLOCK), bf16),
            pltpu.SMEM((blocks,), jnp.int32),
            pltpu.SemaphoreType.DMA((phases,)),
            pltpu.SemaphoreType.DMA((phases,)),
            pltpu.SemaphoreType.DMA((INPUTS,)),
        ],
        compiler_params=pltpu.CompilerParams(
            collective_id=0, has_side_effects=True, vmem_limit_bytes=40 * 2**20
        ),
    )
    moved = call(*inputs)
    out = jax.ShapeDtypeStruct(positions.shape, f32)
    return pl.pallas_call(
        functools.partial(unfold, blocks),
        out_shape=(out, out, out),
        in_specs=[vmem],
        out_specs=(vmem, vmem, vmem),
        compiler_params=pltpu.CompilerParams(vmem_limit_bytes=40 * 2**20),
    )(moved.reshape(9 * blocks, BLOCK))


def solution(mesh):
    both = ("rep", "dom")
    in_specs = (
        P(None, both),
        P(None, both),
        P(both),
        P(both),
        P("rep"),
        P(both, None),
        P(both, None),
        P(both, None),
        P(both, None),
        P(both, None),
    )
    out_specs = (P(None, both), P(None, both), P(None, both))
    return jax.shard_map(
        functools.partial(on_device, mesh.shape["dom"]),
        mesh=mesh,
        in_specs=in_specs,
        out_specs=out_specs,
        check_vma=False,
    )
```
